32 devices in a mesh: gx: 4 (over x, core), gy: 8 (over z, y).
Axes of the slice: x: 2, y: 2, z: 4, core: 2. Of those that a mesh axis runs over, the one named last changes fastest.
Arguments:
- primal_pops: float32 [27, 64, 64, 6], P(None, 'gx', 'gy'), may hold values from 0.2 to 1.8
- tangent_pops: float32 [27, 64, 64, 384], P(None, 'gx', 'gy'), may hold values from -6 to 6
- inflow_pops: float32 [9, 64, 6], replicated, may hold values from 0.2 to 1.8
- inflow_sens: float32 [9, 64, 384], replicated, may hold values from -6 to 6
- w_in: float32 [128, 27], replicated, may hold values from -1.25 to 1.25
- b_in: float32 [128], replicated, may hold values from -3 to 3
- w_mid: float32 [128, 128], replicated, may hold values from -0.5 to 0.5
- b_mid: float32 [128], replicated, may hold values from -3 to 3
- w_out: float32 [27, 128], replicated, may hold values from -0.5 to 0.5
- b_out: float32 [27], replicated, may hold values from -2 to 2
- probe_cells: int32 [32, 32, 4], P(('gx', 'gy')), may hold values from 0 to 767
- probe_counts: int32 [32, 32], P(('gx', 'gy')), may hold values from 0 to 4, as said below
Outputs:
- primal_out: float32 [27, 64, 64, 6], P(None, 'gx', 'gy')
- tangent_out: float32 [27, 64, 64, 384], P(None, 'gx', 'gy')
- jac_rows: float32 [32, 32, 4, 256], P(('gx', 'gy'))
The draws below stay inside these ranges and needn't reach their ends.
Inputs may be any that keep to these rules, and one draw needn't show every extreme that they name: `probe_cells`: a local cell of the holder; slots at or beyond probe_counts for that owner are unused. `probe_counts`: in every draw one owner receives exactly 4 probes from every holder.
All inputs are finite; a program needn't handle non-finite values.
Results may differ from the reference program's by a relative error of at most 0.00011.
Values sent between devices are 32-bit elements; how exact they have to be, the bound alone decides.
A program may use at most 128 MiB of HBM per device.

```python
import jax
import jax.numpy as jnp
import numpy as np
from jax import lax

BX = 16
BY = 8
NZ = 6
K = 64
HID = 128
STEPS = 2
CAP = 4
NX = 64
NY = 64
PEERS = 32
CELLS = 768
N_GY = 8


def draw_probe_counts(key, part):
    counts_drawn = jax.random.randint(jax.random.fold_in(key, 11), (PEERS, PEERS), 0, CAP + 1)
    busiest = jax.random.randint(jax.random.fold_in(key, 12), (), 0, PEERS)
    columns = lax.broadcasted_iota(jnp.int32, (PEERS, PEERS), 1)
    return jnp.where(columns == busiest, CAP, counts_drawn).astype(jnp.int32)


def place_ends(drawn, rng, least, top_value):
    index_at = [jax.random.randint(jax.random.fold_in(rng, axis), (), 0, length) for axis, length in enumerate(drawn.shape)]
    main_axis = drawn.shape.index(max(drawn.shape))
    next_to = index_at[:main_axis] + [(index_at[main_axis] + 1) % drawn.shape[main_axis]] + index_at[main_axis + 1:]
    return drawn.at[tuple(index_at)].set(least).at[tuple(next_to)].set(top_value)


def level_of(stream_key, shape, shards, low, largest):
    def one(axis_at, shards_of):
        heights = jax.random.uniform(jax.random.fold_in(jax.random.fold_in(stream_key, 6), axis_at), (shards_of,), jnp.float32, low / len(shards), largest / len(shards))
        return jnp.repeat(jnp.exp(heights), shape[axis_at] // shards_of).reshape((-1,) + (1,) * (len(shape) - axis_at - 1))

    gain = one(*shards[0])
    for cut in shards[1:]:
        gain = gain * one(*cut)
    return gain


def bell_draw(key, shape, spread, limit, shards=(), kind=jnp.bfloat16):
    factor_of = level_of(key, shape, shards, -0.22, 0.18) if shards else 1.0
    drawn = jax.random.normal(key, shape, jnp.float32) * spread * factor_of
    return jnp.minimum(jnp.maximum(drawn, -limit), limit).astype(kind)


def setup_inputs(seed: int = 0) -> dict:
    arg_keys = jax.random.split(jax.random.key(seed), 13)
    return {
        "primal_pops": jnp.clip(0.2 + 1.5999999 * jax.random.uniform(arg_keys[0], (27, NX, NY, NZ), jnp.float32) ** level_of(arg_keys[0], (27, NX, NY, NZ), ((1, 4), (2, 8)), -0.2, 0.2), 0.2, 1.8),
        "tangent_pops": bell_draw(arg_keys[1], (27, NX, NY, NZ * K), 1.0, 6.0, ((1, 4), (2, 8)), jnp.float32),
        "inflow_pops": jnp.clip(jax.random.uniform(arg_keys[2], (9, NY, NZ), jnp.float32, 0.2, 1.8), 0.2, 1.8),
        "inflow_sens": bell_draw(arg_keys[3], (9, NY, NZ * K), 1.0, 6.0, (), jnp.float32),
        "w_in": bell_draw(arg_keys[4], (HID, 27), 27 ** -0.5, 1.25, (), jnp.float32),
        "b_in": bell_draw(arg_keys[5], (HID,), 0.5, 3.0, (), jnp.float32),
        "w_mid": bell_draw(arg_keys[6], (HID, HID), HID ** -0.5, 0.5, (), jnp.float32),
        "b_mid": bell_draw(arg_keys[7], (HID,), 0.5, 3.0, (), jnp.float32),
        "w_out": bell_draw(arg_keys[8], (27, HID), HID ** -0.5, 0.5, (), jnp.float32),
        "b_out": bell_draw(arg_keys[9], (27,), 0.3, 2.0, (), jnp.float32),
        "probe_cells": place_ends(jax.random.randint(arg_keys[10], (PEERS, PEERS, CAP), 0, CELLS), jax.random.fold_in(arg_keys[10], 1), 0, CELLS - 1).astype(jnp.int32),
        "probe_counts": draw_probe_counts(jax.random.fold_in(arg_keys[12], 71), 0),
    }


precise = lax.Precision.HIGHEST


def lattice_table():
    return np.array([[q // 9 - 1, (q // 3) % 3 - 1, q % 3 - 1] for q in range(27)])


def observe_table():
    lattice = lattice_table()
    return np.concatenate([np.ones((1, 27)), lattice.T], axis=0).astype(np.float32)


def stream_region(post_state, k_width):
    lattice = lattice_table()
    rows_x = post_state.shape[1] - 2
    rows_y = post_state.shape[2] - 2
    result = []
    for q in range(27):
        step_x, step_y, step_z = (int(v) for v in lattice[q])
        shifted = post_state[q, 1 - step_x:1 - step_x + rows_x, 1 - step_y:1 - step_y + rows_y]
        mirror = post_state[26 - q, 1:1 + rows_x, 1:1 + rows_y]
        if step_z == 1:
            shifted = jnp.concatenate([mirror[..., :k_width], shifted[..., :-k_width]], axis=-1)
        elif step_z == -1:
            shifted = jnp.concatenate([shifted[..., k_width:], mirror[..., -k_width:]], axis=-1)
        result.append(shifted)
    return jnp.stack(result)


def ghost_pad(post_state, inflow):
    inflow_layer = jnp.concatenate([jnp.zeros_like(post_state[:18, :1]), inflow[:, None]], axis=0)
    padded = jnp.concatenate([inflow_layer, post_state, post_state[:, -1:]], axis=1)
    return jnp.concatenate([padded[:, :, -1:], padded, padded[:, :, :1]], axis=2)


def collide_row(inputs, w_in, b_in, w_mid, b_mid, w_out, b_out):
    cell_state, tangent_row = inputs
    span_y, z_depth = cell_state.shape[1], cell_state.shape[2]
    k_width = tangent_row.shape[2] // z_depth
    first = jnp.einsum('hq,qyz->hyz', w_in, cell_state, precision=precise) + b_in[:, None, None]
    act_one = jnp.tanh(first)
    second = jnp.einsum('hg,gyz->hyz', w_mid, act_one, precision=precise) + b_mid[:, None, None]
    act_two = jnp.tanh(second)
    new_state = cell_state + jnp.einsum('qh,hyz->qyz', w_out, act_two, precision=precise) + b_out[:, None, None]
    slope_one = 1.0 - act_one * act_one
    slope_two = 1.0 - act_two * act_two
    outer_part = w_out[:, :, None, None] * slope_two[None]
    middle_part = jnp.einsum('qhyz,hg->qgyz', outer_part, w_mid, precision=precise) * slope_one[None]
    cell_matrix = jnp.einsum('qgyz,gp->qpyz', middle_part, w_in, precision=precise)
    tangent_four = tangent_row.reshape(27, span_y, z_depth, k_width)
    new_tangent = tangent_four + jnp.einsum('qpyz,pyzk->qyzk', cell_matrix, tangent_four, precision=precise)
    return new_state, new_tangent.reshape(27, span_y, z_depth * k_width)


def reference(primal_pops, tangent_pops, inflow_pops, inflow_sens, w_in, b_in, w_mid, b_mid, w_out, b_out, probe_cells, probe_counts):
    primal, tangent = primal_pops, tangent_pops
    for step_index in range(STEPS):
        def row_update(inputs):
            return collide_row(inputs, w_in, b_in, w_mid, b_mid, w_out, b_out)
        new_primal, new_tangent = lax.map(row_update, (jnp.moveaxis(primal, 1, 0), jnp.moveaxis(tangent, 1, 0)))
        primal = stream_region(ghost_pad(jnp.moveaxis(new_primal, 0, 1), inflow_pops), 1)
        tangent = stream_region(ghost_pad(jnp.moveaxis(new_tangent, 0, 1), inflow_sens), K)
    observe = jnp.asarray(observe_table(), jnp.float32)
    observed = jnp.einsum('oq,qxyw->oxyw', observe, tangent, precision=precise)
    grid = observed.reshape(4, NX, NY, NZ, K)
    holder = jnp.arange(PEERS, dtype=jnp.int32)[:, None, None]
    place_x = (holder // N_GY) * BX + probe_cells // (BY * NZ)
    place_y = (holder % N_GY) * BY + (probe_cells // NZ) % BY
    place_z = probe_cells % NZ
    picked = grid[:, place_x, place_y, place_z, :]
    ordered = jnp.transpose(picked, (2, 1, 3, 0, 4)).reshape(PEERS, PEERS, CAP, 4 * K)
    slot_index = jnp.arange(CAP, dtype=jnp.int32)[None, None, :]
    live_slot = slot_index < jnp.transpose(probe_counts)[:, :, None]
    jac_rows = jnp.where(live_slot[..., None], ordered, jnp.zeros_like(ordered))
    return primal, tangent, jac_rows
```

```python
import functools

import jax
import jax.numpy as jnp
from jax import lax
from jax.experimental import pallas as pl
from jax.experimental.pallas import tpu as pltpu
from jax.sharding import PartitionSpec as P

STEPS = 2
QS = 32
LANES = 128
GROUP = 6
VMEM_LIMIT = 60 * 1024 * 1024
LATTICE = [(q // 9 - 1, q // 3 % 3 - 1, q % 3 - 1) for q in range(27)]
precise = lax.Precision.HIGHEST


def split(value):
    high = value.astype(jnp.bfloat16)
    low = (value - high.astype(jnp.float32)).astype(jnp.bfloat16)
    return high, low


def dot(a, b):
    return jnp.dot(a, b, preferred_element_type=jnp.float32)


def lane_iota(rows):
    return lax.broadcasted_iota(jnp.int32, (rows, LANES), 1)


def primal_collide(state_ref, weights, post_ref, slope_one_ref, slope_two_ref):
    w_in, b_in, w_mid, b_mid, w_out, b_out = weights
    rows_x = post_ref.shape[1]

    def one(x, carry):
        cell = state_ref[pl.ds(x, QS, stride=rows_x), :]
        first = jnp.dot(w_in[...], cell, precision=precise, preferred_element_type=jnp.float32)
        act_one = jnp.tanh(first + b_in[...])
        second = jnp.dot(w_mid[...], act_one, precision=precise, preferred_element_type=jnp.float32)
        act_two = jnp.tanh(second + b_mid[...])
        moved = jnp.dot(w_out[...], act_two, precision=precise, preferred_element_type=jnp.float32)
        slope_one_ref[x] = 1.0 - act_one * act_one
        slope_two_ref[x] = 1.0 - act_two * act_two
        state_ref[pl.ds(x, QS, stride=rows_x), :] = cell + moved + b_out[...]
        return carry

    lax.fori_loop(0, rows_x, one, 0)
    for q in range(27):
        post_ref[q] = state_ref[q * rows_x : (q + 1) * rows_x, :]


def primal_stream(post_ref, x_low, x_high, y_low, y_high, write, z_depth):
    rows_x, rows_y = post_ref.shape[1], 8
    lane = lane_iota(rows_x)
    at_y = lane % rows_y
    last_z = (z_depth - 1) * rows_y
    for q, (ex, ey, ez) in enumerate(LATTICE):
        own = post_ref[q]
        if ex == 1:
            own = jnp.concatenate([x_low[q - 18], own[: rows_x - 1]], axis=0)
        elif ex == -1:
            own = jnp.concatenate([own[1:], x_high[q]], axis=0)
        if ey != 0:
            j = (ex + 1) * 3 + ez + 1
            side = (y_low if ey == 1 else y_high)[j, 1 - ex : 1 - ex + rows_x]
            if ey == 1:
                own = jnp.where(at_y == 0, pltpu.roll(side, LANES - rows_y + 1, 1), pltpu.roll(own, 1, 1))
            else:
                own = jnp.where(at_y == rows_y - 1, pltpu.roll(side, rows_y - 1, 1), pltpu.roll(own, LANES - 1, 1))
        if ez == 1:
            own = jnp.where(lane < rows_y, post_ref[26 - q], pltpu.roll(own, rows_y, 1))
        elif ez == -1:
            own = jnp.where(lane >= last_z, post_ref[26 - q], pltpu.roll(own, LANES - rows_y, 1))
        write(q, own)


def primal_first(cells, w_in, b_in, w_mid, b_mid, w_out, b_out, post, slope_one, slope_two, state):
    rows_x = cells.shape[1]
    state[...] = jnp.zeros_like(state)
    for q in range(27):
        state[q * rows_x : (q + 1) * rows_x, :] = cells[q]
    primal_collide(state, (w_in, b_in, w_mid, b_mid, w_out, b_out), post, slope_one, slope_two)


def primal_next(z_depth, before, x_low, x_high, y_low, y_high, w_in, b_in, w_mid, b_mid, w_out, b_out,
                post, slope_one, slope_two, state):
    rows_x = before.shape[1]
    state[...] = jnp.zeros_like(state)

    def write(q, value):
        state[q * rows_x : (q + 1) * rows_x, :] = value

    primal_stream(before, x_low, x_high, y_low, y_high, write, z_depth)
    primal_collide(state, (w_in, b_in, w_mid, b_mid, w_out, b_out), post, slope_one, slope_two)


def primal_last(z_depth, before, x_low, x_high, y_low, y_high, out):
    def write(q, value):
        out[q] = value

    primal_stream(before, x_low, x_high, y_low, y_high, write, z_depth)


def make_weights(w_in, w_mid, w_out, one, two, three):
    high, low = split(w_in[...])
    one[...] = jnp.concatenate([high, high, low], axis=1)
    high, low = split(w_mid[...])
    two[...] = jnp.concatenate(
        [jnp.concatenate([high, high], axis=1), jnp.concatenate([low, jnp.zeros_like(low)], axis=1)], axis=0
    )
    high, low = split(w_out[...])
    three[...] = jnp.concatenate(
        [jnp.concatenate([high, high], axis=1), jnp.concatenate([low, jnp.zeros_like(low)], axis=1)], axis=0
    )


def tangent_collide(state, post, faces, slope_one, slope_two, one, two, three):
    rows_x, pairs = state.shape[0], state.shape[1]
    rows_y = 8
    hidden = two.shape[0] // 2
    below, above, side_low, side_high = faces

    def row(x, carry):
        half = lane_iota(hidden) < LANES // 2
        s_one, s_two = slope_one[x], slope_two[x]

        def scale(slopes, y, pair):
            left = slopes[:, 2 * pair * rows_y + y : 2 * pair * rows_y + y + 1]
            right = slopes[:, (2 * pair + 1) * rows_y + y : (2 * pair + 1) * rows_y + y + 1]
            return jnp.where(half, left, right)

        columns = [(y, pair) for y in range(rows_y) for pair in range(pairs)]
        for start in range(0, len(columns), GROUP):
            here = columns[start : start + GROUP]
            cell = jnp.concatenate([state[x, pair, pl.ds(y, QS, stride=rows_y), :] for y, pair in here], axis=1)
            high, low = split(cell)
            lifted = dot(one[...], jnp.concatenate([high, low, high], axis=0))
            high, low = split(lifted * jnp.concatenate([scale(s_one, y, pair) for y, pair in here], axis=1))
            mixed = dot(two[...], jnp.concatenate([high, low], axis=0))
            mixed = mixed[:hidden] + mixed[hidden:]
            high, low = split(mixed * jnp.concatenate([scale(s_two, y, pair) for y, pair in here], axis=1))
            moved = dot(three[...], jnp.concatenate([high, low], axis=0))
            result = cell + moved[:QS] + moved[QS:]
            for i, (y, pair) in enumerate(here):
                post[x, pair, pl.ds(y, QS, stride=rows_y), :] = result[:, i * LANES : (i + 1) * LANES]
        return carry

    lax.fori_loop(0, rows_x, row, 0)
    stride = pairs * QS * rows_y
    flat = post.reshape(rows_x * stride, LANES)
    for pair in range(pairs):
        lanes = slice(pair * LANES, (pair + 1) * LANES)
        for ex in range(3):
            for ez in range(3):
                q = ex * 9 + 6 + ez
                side_high[ex * 3 + ez, :, lanes] = flat[pl.ds((pair * QS + q + 1) * rows_y - 1, rows_x, stride=stride), :]
                q = ex * 9 + ez
                side_low[ex * 3 + ez, :, lanes] = flat[pl.ds((pair * QS + q) * rows_y, rows_x, stride=stride), :]
        for j in range(9):
            below[j, :, lanes] = post[0, pair, j * rows_y : (j + 1) * rows_y, :]
            above[j, :, lanes] = post[rows_x - 1, pair, (18 + j) * rows_y : (19 + j) * rows_y, :]


def stream_rows(before, x_low, x_high, y_low, y_high, sides, write):
    rows_x, pairs = before.shape[0], before.shape[1]
    rows_y = 8
    lane = lane_iota(rows_y)
    left = lane < LANES // 2
    at_y = lax.broadcasted_iota(jnp.int32, (rows_y, LANES), 0)
    for way, given in enumerate((y_low, y_high)):
        for j in range(9):
            for pair in range(pairs):
                sides[way, j, pair, : rows_x + 2] = given[j, :, pair * LANES : (pair + 1) * LANES]

    def one_row(x, edge):
        for q, (ex, ey, ez) in enumerate(LATTICE):
            parts = []
            for pair in range(pairs):
                lanes = slice(pair * LANES, (pair + 1) * LANES)
                if edge == -1 and ex == 1:
                    value = x_low[q - 18, :, lanes]
                elif edge == 1 and ex == -1:
                    value = x_high[q, :, lanes]
                else:
                    value = before[x - ex, pair, q * rows_y : (q + 1) * rows_y, :]
                if ey != 0:
                    j = (ex + 1) * 3 + ez + 1
                    side = sides[0 if ey == 1 else 1, j, pair, pl.ds(x - ex + 1, 1), :]
                    if ey == 1:
                        value = jnp.where(at_y == 0, side, pltpu.roll(value, 1, 0))
                    else:
                        value = jnp.where(at_y == rows_y - 1, side, pltpu.roll(value, rows_y - 1, 0))
                parts.append(value)
            if ez != 0:
                turned = [pltpu.roll(part, LANES // 2, 1) for part in parts]
                mirror = 26 - q
                if ez == 1:
                    wall = before[x, 0, mirror * rows_y : (mirror + 1) * rows_y, :]
                    parts = [jnp.where(left, turned[p - 1] if p else wall, turned[p]) for p in range(pairs)]
                else:
                    wall = before[x, pairs - 1, mirror * rows_y : (mirror + 1) * rows_y, :]
                    parts = [jnp.where(left, turned[p], turned[p + 1] if p + 1 < pairs else wall) for p in range(pairs)]
            write(x, q, parts)

    one_row(0, -1)

    def inner(x, carry):
        one_row(x, 0)
        return carry

    lax.fori_loop(1, rows_x - 1, inner, 0)
    one_row(rows_x - 1, 1)


def tangent_first(cells, slope_one, slope_two, w_in, w_mid, w_out, post, below, above, side_low, side_high,
                  state, one, two, three):
    rows_x, pairs = state.shape[0], state.shape[1]
    make_weights(w_in, w_mid, w_out, one, two, three)

    def load(x, carry):
        for pair in range(pairs):
            for q in range(27):
                state[x, pair, q * 8 : (q + 1) * 8, :] = cells[q, x, :, pair * LANES : (pair + 1) * LANES]
            state[x, pair, 27 * 8 :, :] = jnp.zeros((5 * 8, LANES), jnp.float32)
        return carry

    lax.fori_loop(0, rows_x, load, 0)
    tangent_collide(state, post, (below, above, side_low, side_high), slope_one, slope_two, one, two, three)


def tangent_next(before, x_low, x_high, y_low, y_high, slope_one, slope_two, w_in, w_mid, w_out,
                 post, below, above, side_low, side_high, state, one, two, three, sides):
    rows_x, pairs = state.shape[0], state.shape[1]
    make_weights(w_in, w_mid, w_out, one, two, three)

    def write(x, q, parts):
        for pair in range(pairs):
            state[x, pair, q * 8 : (q + 1) * 8, :] = parts[pair]
            if q == 0:
                state[x, pair, 27 * 8 :, :] = jnp.zeros((5 * 8, LANES), jnp.float32)

    stream_rows(before, x_low, x_high, y_low, y_high, sides, write)
    tangent_collide(state, post, (below, above, side_low, side_high), slope_one, slope_two, one, two, three)


def tangent_last(z_depth, probe_cells, probe_counts, before, x_low, x_high, y_low, y_high, out, rows_out, observed, sides):
    pairs = before.shape[1]
    rows_y = 8
    sums = {}

    def write(x, q, parts):
        vector = LATTICE[q]
        for pair in range(pairs):
            out[q, x, :, pair * LANES : (pair + 1) * LANES] = parts[pair]
            held = sums.setdefault((pair,), [None] * 4) if q else sums.__setitem__((pair,), [None] * 4) or sums[(pair,)]
            for m, factor in enumerate((1,) + vector):
                if factor == 0:
                    continue
                if held[m] is None:
                    held[m] = parts[pair] if factor == 1 else -parts[pair]
                else:
                    held[m] = held[m] + parts[pair] if factor == 1 else held[m] - parts[pair]
            if q == 26:
                for m in range(4):
                    observed[m, pair, pl.ds(pl.multiple_of(x * rows_y, rows_y), rows_y), :] = held[m]

    stream_rows(before, x_low, x_high, y_low, y_high, sides, write)
    peers, slots = probe_cells.shape
    left = lane_iota(1) < LANES // 2

    def probe(peer, carry):
        for slot in range(slots):
            cell = jnp.clip(probe_cells[peer, slot], 0, observed.shape[2] * z_depth - 1)
            place, z = cell // z_depth, cell % z_depth
            pair, odd = z // 2, z % 2
            live = slot < probe_counts[0, peer]
            rows = [observed[m, pair, pl.ds(place, 1), :] for m in range(4)]
            turned = [pltpu.roll(r, LANES // 2, 1) for r in rows]
            for m in (0, 2):
                low = jnp.where(odd == 1, turned[m], rows[m])
                high = jnp.where(odd == 1, rows[m + 1], turned[m + 1])
                value = jnp.where(left, low, high)
                rows_out[peer, slot : slot + 1, m * 64 : m * 64 + LANES] = jnp.where(live, value, 0.0)
        return carry

    lax.fori_loop(0, peers, probe, 0, unroll=2)


def shifts(axis, wrap):
    n = lax.axis_size(axis)
    up = [(i, (i + 1) % n) for i in range(n if wrap else n - 1)]
    return up, [(j, i) for i, j in up]


def spread(first, last, sides):
    x_low, x_high = first
    low_corner, high_corner, side_low, side_high = last
    up, down = sides
    pad = jnp.zeros((6, 1) + side_low.shape[2:], side_low.dtype)

    def full(side, low, high):
        return jnp.concatenate(
            [jnp.concatenate([pad, low], axis=0), side, jnp.concatenate([high, pad], axis=0)], axis=1
        )

    y_low = lax.ppermute(full(side_high, low_corner[0], high_corner[0]), "gy", up)
    y_high = lax.ppermute(full(side_low, low_corner[1], high_corner[1]), "gy", down)
    return x_low, x_high, y_low, y_high


def edge_rows(below, above, inflow, own_last):
    column, columns = lax.axis_index("gx"), lax.axis_size("gx")
    up, down = shifts("gx", False)
    x_low = jnp.where(column == 0, inflow, lax.ppermute(above, "gx", up))
    x_high = jnp.where(column == columns - 1, own_last, lax.ppermute(below, "gx", down))
    return x_low, x_high


def primal_halo(post, inflow):
    rows_x = post.shape[1]
    x_low, x_high = edge_rows(post[:9, :1], post[18:, rows_x - 1 :], inflow, post[:9, rows_x - 1 :])
    cut = post.reshape((3, 3, 3) + post.shape[1:])
    side = [cut[:, way].reshape((9,) + post.shape[1:]) for way in (0, 2)]
    return spread(
        (x_low, x_high), ((x_low[6:], x_low[:3]), (x_high[6:], x_high[:3]), side[0], side[1]), shifts("gy", True)
    )


def tangent_halo(last_row, below, above, side_low, side_high, inflow):
    x_low, x_high = edge_rows(below, above, inflow, last_row)
    return spread(
        (x_low, x_high),
        ((x_low[6:, -1:], x_low[:3, :1]), (x_high[6:, -1:], x_high[:3, :1]), side_low, side_high),
        shifts("gy", True),
    )


def shape(*dims):
    return jax.ShapeDtypeStruct(dims, jnp.float32)


def call(body, outs, scratch=(), specs=None, cost=None, **more):
    return pl.pallas_call(
        body,
        out_shape=outs,
        **({} if specs is None else {"in_specs": specs}),
        scratch_shapes=list(scratch),
        compiler_params=pltpu.CompilerParams(vmem_limit_bytes=VMEM_LIMIT),
        cost_estimate=cost,
        **more,
    )


def on_device(primal_pops, tangent_pops, inflow_pops, inflow_sens, w_in, b_in, w_mid, b_mid, w_out, b_out,
              probe_cells, probe_counts):
    rows_x, rows_y, z_depth = primal_pops.shape[1:]
    width = tangent_pops.shape[3]
    pairs = width // LANES
    hidden = w_in.shape[0]
    row_at = lax.axis_index("gy") * rows_y

    w_in = jnp.pad(w_in, ((0, 0), (0, QS - 27)))
    w_out = jnp.pad(w_out, ((0, QS - 27), (0, 0)))
    weights = (w_in, b_in[:, None], w_mid, b_mid[:, None], w_out, jnp.pad(b_out, (0, QS - 27))[:, None])
    tall = ((0, 0), (0, 0), (0, LANES - z_depth * rows_y))
    cells = jnp.pad(jnp.swapaxes(primal_pops, 2, 3).reshape(27, rows_x, z_depth * rows_y), tall)
    inflow = lax.dynamic_slice_in_dim(inflow_pops, row_at, rows_y, 1)
    inflow = jnp.pad(jnp.swapaxes(inflow, 1, 2).reshape(9, 1, z_depth * rows_y), tall)
    sens = lax.dynamic_slice_in_dim(inflow_sens, row_at, rows_y, 1)

    primal_outs = (shape(27, rows_x, LANES), shape(rows_x, hidden, LANES), shape(rows_x, hidden, LANES))
    primal_scratch = [pltpu.VMEM((QS * rows_x, LANES), jnp.float32)]
    tangent_outs = (
        shape(rows_x, pairs, QS * rows_y, LANES),
        shape(9, rows_y, width),
        shape(9, rows_y, width),
        shape(9, rows_x, width),
        shape(9, rows_x, width),
    )
    tangent_scratch = [
        pltpu.VMEM((rows_x, pairs, QS * rows_y, LANES), jnp.float32),
        pltpu.VMEM((hidden, 3 * QS), jnp.bfloat16),
        pltpu.VMEM((2 * hidden, 2 * hidden), jnp.bfloat16),
        pltpu.VMEM((2 * QS, 2 * hidden), jnp.bfloat16),
    ]
    sides = pltpu.VMEM((2, 9, pairs, rows_x + 8, LANES), jnp.float32)
    cost = pl.CostEstimate(flops=40 * 10**9, bytes_accessed=20 * 10**6, transcendentals=0)

    post, slope_one, slope_two = call(primal_first, primal_outs, primal_scratch)(cells, *weights)
    tangent = call(tangent_first, tangent_outs, tangent_scratch, cost=cost)(
        tangent_pops, slope_one, slope_two, w_in, w_mid, w_out
    )
    for step in range(1, STEPS):
        post, slope_one, slope_two = call(
            functools.partial(primal_next, z_depth), primal_outs, primal_scratch
        )(post, *primal_halo(post, inflow), *weights)
        state, *faces = tangent
        halo = tangent_halo(last_row(state, rows_x, rows_y), *faces, sens)
        tangent = call(tangent_next, tangent_outs, tangent_scratch + [sides], cost=cost)(
            state, *halo, slope_one, slope_two, w_in, w_mid, w_out
        )
    primal = call(functools.partial(primal_last, z_depth), shape(27, rows_x, LANES))(
        post, *primal_halo(post, inflow)
    )
    primal = jnp.swapaxes(primal[:, :, : z_depth * rows_y].reshape(27, rows_x, z_depth, rows_y), 2, 3)
    state, *faces = tangent
    halo = tangent_halo(last_row(state, rows_x, rows_y), *faces, sens)
    peers, slots = probe_cells.shape[1:]
    smem = pl.BlockSpec(memory_space=pltpu.SMEM)
    vmem = pl.BlockSpec(memory_space=pltpu.VMEM)
    tangent, jac = call(
        functools.partial(tangent_last, z_depth),
        (shape(27, rows_x, rows_y, width), shape(peers, slots, 4 * width // z_depth)),
        [pltpu.VMEM((4, pairs, rows_x * rows_y, LANES), jnp.float32), sides],
        specs=[smem, smem] + [vmem] * 5,
    )(probe_cells[0], probe_counts, state, *halo)
    jac = lax.all_to_all(jac[None], ("gx", "gy"), split_axis=1, concat_axis=1, tiled=True)
    return primal, tangent, jac


def last_row(state, rows_x, rows_y):
    row = state[rows_x - 1, :, : 9 * rows_y]
    return jnp.transpose(row.reshape(-1, 9, rows_y, LANES), (1, 2, 0, 3)).reshape(9, rows_y, -1)


def solution(mesh):
    both = P(("gx", "gy"))
    split_xy = P(None, "gx", "gy", None)
    return jax.shard_map(
        on_device,
        mesh=mesh,
        in_specs=(split_xy, split_xy) + (P(),) * 8 + (both, both),
        out_specs=(split_xy, split_xy, both),
        check_vma=False,
    )
```

```python
import functools

import jax
import jax.numpy as jnp
from jax import lax
from jax.experimental import pallas as pl
from jax.experimental.pallas import tpu as pltpu
from jax.sharding import PartitionSpec as P

STEPS = 2
QS = 32
LANES = 128
GROUP = 6
VMEM_LIMIT = 60 * 1024 * 1024
LATTICE = [(q // 9 - 1, q // 3 % 3 - 1, q % 3 - 1) for q in range(27)]


def split(value):
    high = value.astype(jnp.bfloat16)
    low = (value - high.astype(jnp.float32)).astype(jnp.bfloat16)
    return high, low


def dot(a, b):
    return jnp.dot(a, b, preferred_element_type=jnp.float32)


def lane_iota(rows):
    return lax.broadcasted_iota(jnp.int32, (rows, LANES), 1)


def make_weights(w_in, w_mid, w_out, one, two, three):
    high, low = split(w_in[...])
    one[...] = jnp.concatenate([high, high, low], axis=1)
    high, low = split(w_mid[...])
    two[...] = jnp.concatenate(
        [jnp.concatenate([high, high], axis=1), jnp.concatenate([low, jnp.zeros_like(low)], axis=1)], axis=0
    )
    high, low = split(w_out[...])
    three[...] = jnp.concatenate(
        [jnp.concatenate([high, high], axis=1), jnp.concatenate([low, jnp.zeros_like(low)], axis=1)], axis=0
    )


def primal_stream(post_ref, x_rows, y_sides, write, z_depth):
    rows_x, rows_y = post_ref.shape[1], 8
    lane = lane_iota(rows_x)
    at_y = lane % rows_y
    last_z = (z_depth - 1) * rows_y
    for q, (ex, ey, ez) in enumerate(LATTICE):
        own = post_ref[q]
        if ex == 1:
            own = jnp.concatenate([x_rows[0, q - 18 : q - 17, :], own[: rows_x - 1]], axis=0)
        elif ex == -1:
            own = jnp.concatenate([own[1:], x_rows[1, q : q + 1, :]], axis=0)
        if ey != 0:
            j = (ex + 1) * 3 + ez + 1
            side = y_sides[0 if ey == 1 else 1, j, 1 - ex : 1 - ex + rows_x, :]
            if ey == 1:
                own = jnp.where(at_y == 0, pltpu.roll(side, LANES - rows_y + 1, 1), pltpu.roll(own, 1, 1))
            else:
                own = jnp.where(at_y == rows_y - 1, pltpu.roll(side, rows_y - 1, 1), pltpu.roll(own, LANES - 1, 1))
        if ez == 1:
            own = jnp.where(lane < rows_y, post_ref[26 - q], pltpu.roll(own, rows_y, 1))
        elif ez == -1:
            own = jnp.where(lane >= last_z, post_ref[26 - q], pltpu.roll(own, LANES - rows_y, 1))
        write(q, own)


def stream_rows(before, x_rows, sides, write):
    rows_x, pairs = before.shape[0], before.shape[1]
    rows_y = 8
    lane = lane_iota(rows_y)
    left = lane < LANES // 2
    at_y = lax.broadcasted_iota(jnp.int32, (rows_y, LANES), 0)
    def one_row(x, edge):
        for q, (ex, ey, ez) in enumerate(LATTICE):
            parts = []
            for pair in range(pairs):
                if edge == -1 and ex == 1:
                    value = x_rows[0, q - 18, pair]
                elif edge == 1 and ex == -1:
                    value = x_rows[1, q, pair]
                else:
                    value = before[x - ex, pair, q * rows_y : (q + 1) * rows_y, :]
                if ey != 0:
                    j = (ex + 1) * 3 + ez + 1
                    side = sides[0 if ey == 1 else 1, j, pair, pl.ds(x - ex + 1, 1), :]
                    if ey == 1:
                        value = jnp.where(at_y == 0, side, pltpu.roll(value, 1, 0))
                    else:
                        value = jnp.where(at_y == rows_y - 1, side, pltpu.roll(value, rows_y - 1, 0))
                parts.append(value)
            if ez != 0:
                turned = [pltpu.roll(part, LANES // 2, 1) for part in parts]
                mirror = 26 - q
                if ez == 1:
                    wall = before[x, 0, mirror * rows_y : (mirror + 1) * rows_y, :]
                    parts = [jnp.where(left, turned[p - 1] if p else wall, turned[p]) for p in range(pairs)]
                else:
                    wall = before[x, pairs - 1, mirror * rows_y : (mirror + 1) * rows_y, :]
                    parts = [jnp.where(left, turned[p], turned[p + 1] if p + 1 < pairs else wall) for p in range(pairs)]
            write(x, q, parts)

    one_row(0, -1)

    def inner(x, carry):
        one_row(x, 0)
        return carry

    lax.fori_loop(1, rows_x - 1, inner, 0)
    one_row(rows_x - 1, 1)


def primal_collide(state_ref, biases, post_ref, slope_one_ref, slope_two_ref, one, two, three):
    b_in, b_mid, b_out = biases
    rows_x = post_ref.shape[1]
    hidden = two.shape[0] // 2

    def row(x, carry):
        cell = state_ref[pl.ds(x, QS, stride=rows_x), :]
        high, low = split(cell)
        act_one = jnp.tanh(dot(one[...], jnp.concatenate([high, low, high], axis=0)) + b_in[...])
        high, low = split(act_one)
        second = dot(two[...], jnp.concatenate([high, low], axis=0))
        act_two = jnp.tanh(second[:hidden] + second[hidden:] + b_mid[...])
        high, low = split(act_two)
        moved = dot(three[...], jnp.concatenate([high, low], axis=0))
        slope_one_ref[x] = 1.0 - act_one * act_one
        slope_two_ref[x] = 1.0 - act_two * act_two
        state_ref[pl.ds(x, QS, stride=rows_x), :] = cell + moved[:QS] + moved[QS:] + b_out[...]
        return carry

    lax.fori_loop(0, rows_x, row, 0, unroll=4)
    for q in range(27):
        post_ref[q] = state_ref[q * rows_x : (q + 1) * rows_x, :]


def collide_columns(x, columns, state, post, slope_one, slope_two, one, two, three):
    rows_y = 8
    hidden = two.shape[0] // 2
    half = lane_iota(hidden) < LANES // 2
    s_one, s_two = slope_one[x], slope_two[x]

    def scale(slopes, y, pair):
        left = slopes[:, 2 * pair * rows_y + y : 2 * pair * rows_y + y + 1]
        right = slopes[:, (2 * pair + 1) * rows_y + y : (2 * pair + 1) * rows_y + y + 1]
        return jnp.where(half, left, right)

    for start in range(0, len(columns), GROUP):
        here = columns[start : start + GROUP]
        cell = jnp.concatenate([state[x, pair, pl.ds(y, QS, stride=rows_y), :] for y, pair in here], axis=1)
        high, low = split(cell)
        lifted = dot(one[...], jnp.concatenate([high, low, high], axis=0))
        high, low = split(lifted * jnp.concatenate([scale(s_one, y, pair) for y, pair in here], axis=1))
        mixed = dot(two[...], jnp.concatenate([high, low], axis=0))
        mixed = mixed[:hidden] + mixed[hidden:]
        high, low = split(mixed * jnp.concatenate([scale(s_two, y, pair) for y, pair in here], axis=1))
        moved = dot(three[...], jnp.concatenate([high, low], axis=0))
        result = cell + moved[:QS] + moved[QS:]
        for i, (y, pair) in enumerate(here):
            post[x, pair, pl.ds(y, QS, stride=rows_y), :] = result[:, i * LANES : (i + 1) * LANES]


def exchange_and_collide(cell_state, state, weights, inflow, outs, scratch):
    w_in, b_in, w_mid, b_mid, w_out, b_out = weights
    cell_inflow, sens_inflow = inflow
    cell_post, cell_rows, cell_sides, post, x_rows, sides = outs
    (slope_one, slope_two, one, two, three, cell_edge, cell_face, edge, face,
     cell_edge_in, cell_face_in, cell_corner_in, edge_in, face_in, corner_in, send_sem, recv_sem) = scratch
    rows_x, pairs, rows_y = state.shape[0], state.shape[1], 8
    column, columns_x = lax.axis_index("gx"), lax.axis_size("gx")
    line, lines = lax.axis_index("gy"), lax.axis_size("gy")

    def at(dx, dy):
        return (lax.rem(column + dx + columns_x, columns_x), lax.rem(line + dy + lines, lines))

    barrier = pltpu.get_barrier_semaphore()
    for dx in (-1, 0, 1):
        for dy in (-1, 0, 1):
            if dx or dy:
                pl.semaphore_signal(barrier, inc=1, device_id=at(dx, dy), device_id_type=pl.DeviceIdType.MESH)

    copies = []

    def send(source, target, dx, dy):
        i = len(copies)
        copy = pltpu.make_async_remote_copy(
            src_ref=source, dst_ref=target, send_sem=send_sem.at[i], recv_sem=recv_sem.at[i],
            device_id=at(dx, dy), device_id_type=pl.DeviceIdType.MESH,
        )
        copy.start()
        copies.append(copy)

    make_weights(w_in, w_mid, w_out, one, two, three)
    primal_collide(cell_state, (b_in, b_mid, b_out), cell_post, slope_one, slope_two, one, two, three)
    cell_edge[0] = cell_state[pl.ds(0, 16, stride=rows_x), :]
    cell_edge[1, :9] = cell_state[pl.ds(18 * rows_x + rows_x - 1, 9, stride=rows_x), :]
    cell_edge[1, 9:] = jnp.zeros((7, LANES), jnp.float32)
    for ex in range(3):
        for ez in range(3):
            cell_face[1, ex * 3 + ez] = cell_post[ex * 9 + 6 + ez]
            cell_face[0, ex * 3 + ez] = cell_post[ex * 9 + ez]

    inner = [(y, pair) for y in range(1, rows_y - 1) for pair in range(pairs)]
    outer = [(y, pair) for y in (0, rows_y - 1) for pair in range(pairs)]

    def outer_row(x, carry):
        collide_columns(x, outer, state, post, slope_one, slope_two, one, two, three)
        return carry

    def inner_row(x, carry):
        collide_columns(x, inner, state, post, slope_one, slope_two, one, two, three)
        return carry

    def end_row(i, carry):
        return inner_row(i * (rows_x - 1), carry)

    lax.fori_loop(0, rows_x, outer_row, 0, unroll=4)
    lax.fori_loop(0, 2, end_row, 0)
    stride = pairs * QS * rows_y
    flat = post.reshape(rows_x * stride, LANES)
    for pair in range(pairs):
        for ex in range(3):
            for ez in range(3):
                q = ex * 9 + 6 + ez
                face[1, ex * 3 + ez, pair] = flat[pl.ds((pair * QS + q + 1) * rows_y - 1, rows_x, stride=stride), :]
                q = ex * 9 + ez
                face[0, ex * 3 + ez, pair] = flat[pl.ds((pair * QS + q) * rows_y, rows_x, stride=stride), :]
        for j in range(9):
            edge[0, j, pair] = post[0, pair, j * rows_y : (j + 1) * rows_y, :]
            edge[1, j, pair] = post[rows_x - 1, pair, (18 + j) * rows_y : (19 + j) * rows_y, :]

    pl.semaphore_wait(barrier, 8)
    send(face.at[1], face_in.at[0], 0, 1)
    send(face.at[0], face_in.at[1], 0, -1)
    send(edge.at[1], edge_in.at[0], 1, 0)
    send(edge.at[0], edge_in.at[1], -1, 0)
    send(edge.at[1, 6:9], corner_in.at[0], 1, 1)
    send(edge.at[0, 6:9], corner_in.at[1], -1, 1)
    send(edge.at[1, 0:3], corner_in.at[2], 1, -1)
    send(edge.at[0, 0:3], corner_in.at[3], -1, -1)
    send(cell_face.at[1], cell_face_in.at[0], 0, 1)
    send(cell_face.at[0], cell_face_in.at[1], 0, -1)
    send(cell_edge.at[1], cell_edge_in.at[0], 1, 0)
    send(cell_edge.at[0], cell_edge_in.at[1], -1, 0)
    send(cell_edge.at[1], cell_corner_in.at[0], 1, 1)
    send(cell_edge.at[0], cell_corner_in.at[1], -1, 1)
    send(cell_edge.at[1], cell_corner_in.at[2], 1, -1)
    send(cell_edge.at[0], cell_corner_in.at[3], -1, -1)

    lax.fori_loop(1, rows_x - 1, inner_row, 0)
    for copy in copies:
        copy.wait()

    first, last = column == 0, column == columns_x - 1
    end = rows_x + 1
    cell_rows[0] = jnp.where(first, cell_inflow[1], cell_edge_in[0])
    cell_rows[1] = jnp.where(last, cell_state[pl.ds(rows_x - 1, 16, stride=rows_x), :], cell_edge_in[1])
    for j in range(9):
        for way in range(2):
            cell_sides[way, j, 1:end] = cell_face_in[way, j]
        for pair in range(pairs):
            own = post[rows_x - 1, pair, j * rows_y : (j + 1) * rows_y, :]
            x_rows[0, j, pair] = jnp.where(first, sens_inflow[1, j, pair], edge_in[0, j, pair])
            x_rows[1, j, pair] = jnp.where(last, own, edge_in[1, j, pair])
            for way in range(2):
                sides[way, j, pair, 1:end] = face_in[way, j, pair]
    for way, take in ((0, 6), (1, 0)):
        y = rows_y - 1 if way == 0 else 0
        for i in range(3):
            k = take + i
            cell_sides[way, 6 + i, 0:1] = jnp.where(
                first, cell_inflow[2 * way, k : k + 1, :], cell_corner_in[2 * way, k : k + 1, :])
            cell_sides[way, i, end : end + 1] = jnp.where(
                last, cell_face_in[way, i, rows_x - 1 :, :], cell_corner_in[2 * way + 1, k : k + 1, :])
            for pair in range(pairs):
                sides[way, 6 + i, pair, 0:1] = jnp.where(
                    first, sens_inflow[2 * way, k, pair, y : y + 1, :], corner_in[2 * way, i, pair, y : y + 1, :])
                sides[way, i, pair, end : end + 1] = jnp.where(
                    last, face_in[way, i, pair, rows_x - 1 :, :], corner_in[2 * way + 1, i, pair, y : y + 1, :])


def first_step(cells, tangent, cell_inflow, sens_inflow, w_in, b_in, w_mid, b_mid, w_out, b_out, *rest):
    outs, (cell_state, state), scratch = rest[:6], rest[6:8], rest[8:]
    rows_x, pairs = state.shape[0], state.shape[1]
    cell_state[27 * rows_x :, :] = jnp.zeros((5 * rows_x, LANES), jnp.float32)
    for q in range(27):
        cell_state[q * rows_x : (q + 1) * rows_x, :] = cells[q]

    def load(x, carry):
        for pair in range(pairs):
            for q in range(27):
                state[x, pair, q * 8 : (q + 1) * 8, :] = tangent[q, x, :, pair * LANES : (pair + 1) * LANES]
            state[x, pair, 27 * 8 :, :] = jnp.zeros((5 * 8, LANES), jnp.float32)
        return carry

    lax.fori_loop(0, rows_x, load, 0)
    weights = (w_in, b_in, w_mid, b_mid, w_out, b_out)
    exchange_and_collide(cell_state, state, weights, (cell_inflow, sens_inflow), outs, scratch)


def next_step(z_depth, cells, cell_rows, cell_sides, before, x_rows, sides, cell_inflow, sens_inflow,
              w_in, b_in, w_mid, b_mid, w_out, b_out, *rest):
    outs, (cell_state, state), scratch = rest[:6], rest[6:8], rest[8:]
    rows_x, pairs = state.shape[0], state.shape[1]
    cell_state[27 * rows_x :, :] = jnp.zeros((5 * rows_x, LANES), jnp.float32)

    def keep(q, value):
        cell_state[q * rows_x : (q + 1) * rows_x, :] = value

    primal_stream(cells, cell_rows, cell_sides, keep, z_depth)

    def write(x, q, parts):
        for pair in range(pairs):
            state[x, pair, q * 8 : (q + 1) * 8, :] = parts[pair]
            if q == 0:
                state[x, pair, 27 * 8 :, :] = jnp.zeros((5 * 8, LANES), jnp.float32)

    stream_rows(before, x_rows, sides, write)
    weights = (w_in, b_in, w_mid, b_mid, w_out, b_out)
    exchange_and_collide(cell_state, state, weights, (cell_inflow, sens_inflow), outs, scratch)


def last_step(z_depth, probe_cells, probe_counts, cells, cell_rows, cell_sides, before, x_rows, sides, primal_out, out, rows_out, observed):
    pairs = before.shape[1]
    rows_y = 8
    sums = {}

    def write(x, q, parts):
        vector = LATTICE[q]
        for pair in range(pairs):
            out[q, x, :, pair * LANES : (pair + 1) * LANES] = parts[pair]
            held = sums.setdefault((pair,), [None] * 4) if q else sums.__setitem__((pair,), [None] * 4) or sums[(pair,)]
            for m, factor in enumerate((1,) + vector):
                if factor == 0:
                    continue
                if held[m] is None:
                    held[m] = parts[pair] if factor == 1 else -parts[pair]
                else:
                    held[m] = held[m] + parts[pair] if factor == 1 else held[m] - parts[pair]
            if q == 26:
                for m in range(4):
                    observed[m, pair, pl.ds(pl.multiple_of(x * rows_y, rows_y), rows_y), :] = held[m]

    def keep(q, value):
        primal_out[q] = value

    primal_stream(cells, cell_rows, cell_sides, keep, z_depth)
    stream_rows(before, x_rows, sides, write)
    peers, slots = probe_cells.shape
    left = lane_iota(1) < LANES // 2

    def probe(peer, carry):
        for slot in range(slots):
            cell = jnp.clip(probe_cells[peer, slot], 0, observed.shape[2] * z_depth - 1)
            place, z = cell // z_depth, cell % z_depth
            pair, odd = z // 2, z % 2
            live = slot < probe_counts[0, peer]
            rows = [observed[m, pair, pl.ds(place, 1), :] for m in range(4)]
            turned = [pltpu.roll(r, LANES // 2, 1) for r in rows]
            for m in (0, 2):
                low = jnp.where(odd == 1, turned[m], rows[m])
                high = jnp.where(odd == 1, rows[m + 1], turned[m + 1])
                value = jnp.where(left, low, high)
                rows_out[peer, slot : slot + 1, m * 64 : m * 64 + LANES] = jnp.where(live, value, 0.0)
        return carry

    lax.fori_loop(0, peers, probe, 0, unroll=2)


def shape(*dims):
    return jax.ShapeDtypeStruct(dims, jnp.float32)


def call(body, outs, scratch=(), collective=None, **more):
    params = {} if collective is None else {"collective_id": collective, "has_side_effects": True}
    return pl.pallas_call(
        body,
        out_shape=outs,
        scratch_shapes=list(scratch),
        compiler_params=pltpu.CompilerParams(vmem_limit_bytes=VMEM_LIMIT, **params),
        **more,
    )


def near_inflow(values, row_at, rows_y):
    around = jnp.concatenate([values[:, -rows_y:], values, values[:, :rows_y]], axis=1)
    return lax.dynamic_slice_in_dim(around, row_at, 3 * rows_y, 1).reshape(9, 3, rows_y, -1)


def on_device(primal_pops, tangent_pops, inflow_pops, inflow_sens, w_in, b_in, w_mid, b_mid, w_out, b_out,
              probe_cells, probe_counts):
    rows_x, rows_y, z_depth = primal_pops.shape[1:]
    width = tangent_pops.shape[3]
    pairs = width // LANES
    hidden = w_in.shape[0]
    row_at = lax.axis_index("gy") * rows_y

    w_in = jnp.pad(w_in, ((0, 0), (0, QS - 27)))
    w_out = jnp.pad(w_out, ((0, QS - 27), (0, 0)))
    weights = (w_in, b_in[:, None], w_mid, b_mid[:, None], w_out, jnp.pad(b_out, (0, QS - 27))[:, None])
    tall = ((0, 0), (0, 0), (0, LANES - z_depth * rows_y))
    cells = jnp.pad(jnp.swapaxes(primal_pops, 2, 3).reshape(27, rows_x, z_depth * rows_y), tall)
    inflow = jnp.transpose(near_inflow(inflow_pops, row_at, rows_y), (1, 0, 3, 2)).reshape(3, 9, z_depth * rows_y)
    inflow = jnp.pad(inflow, ((0, 0), (0, 7), (0, LANES - z_depth * rows_y)))
    sens = near_inflow(inflow_sens, row_at, rows_y).reshape(9, 3, rows_y, pairs, LANES)
    sens = jnp.transpose(sens, (1, 0, 3, 2, 4))

    tall_x = rows_x + 8
    outs = (
        shape(27, rows_x, LANES),
        shape(2, 16, LANES),
        shape(2, 9, tall_x, LANES),
        shape(rows_x, pairs, QS * rows_y, LANES),
        shape(2, 9, pairs, rows_y, LANES),
        shape(2, 9, pairs, tall_x, LANES),
    )

    def room(*dims, kind=jnp.float32):
        return pltpu.VMEM(dims, kind)

    scratch = [
        room(QS * rows_x, LANES),
        room(rows_x, pairs, QS * rows_y, LANES),
        room(rows_x, hidden, LANES),
        room(rows_x, hidden, LANES),
        room(hidden, 3 * QS, kind=jnp.bfloat16),
        room(2 * hidden, 2 * hidden, kind=jnp.bfloat16),
        room(2 * QS, 2 * hidden, kind=jnp.bfloat16),
        room(2, 16, LANES),
        room(2, 9, rows_x, LANES),
        room(2, 9, pairs, rows_y, LANES),
        room(2, 9, pairs, rows_x, LANES),
        room(2, 16, LANES),
        room(2, 9, rows_x, LANES),
        room(4, 16, LANES),
        room(2, 9, pairs, rows_y, LANES),
        room(2, 9, pairs, rows_x, LANES),
        room(4, 3, pairs, rows_y, LANES),
        pltpu.SemaphoreType.DMA((16,)),
        pltpu.SemaphoreType.DMA((16,)),
    ]
    held = call(first_step, outs, scratch, 1)(cells, tangent_pops, inflow, sens, *weights)
    for step in range(1, STEPS):
        held = call(functools.partial(next_step, z_depth), outs, scratch, 1 + step)(*held, inflow, sens, *weights)
    peers, slots = probe_cells.shape[1:]
    smem = pl.BlockSpec(memory_space=pltpu.SMEM)
    vmem = pl.BlockSpec(memory_space=pltpu.VMEM)
    primal, tangent, jac = call(
        functools.partial(last_step, z_depth),
        (
            shape(27, rows_x, LANES),
            shape(27, rows_x, rows_y, width),
            shape(peers, slots, 4 * width // z_depth),
        ),
        [room(4, pairs, rows_x * rows_y, LANES)],
        in_specs=[smem, smem] + [vmem] * 6,
    )(probe_cells[0], probe_counts, *held)
    primal = jnp.swapaxes(primal[:, :, : z_depth * rows_y].reshape(27, rows_x, z_depth, rows_y), 2, 3)
    jac = lax.all_to_all(jac[None], ("gx", "gy"), split_axis=1, concat_axis=1, tiled=True)
    return primal, tangent, jac


def solution(mesh):
    both = P(("gx", "gy"))
    split_xy = P(None, "gx", "gy", None)
    return jax.shard_map(
        on_device,
        mesh=mesh,
        in_specs=(split_xy, split_xy) + (P(),) * 8 + (both, both),
        out_specs=(split_xy, split_xy, both),
        check_vma=False,
    )
```

```python
import functools

import jax
import jax.numpy as jnp
from jax import lax
from jax.experimental import pallas as pl
from jax.experimental.pallas import tpu as pltpu
from jax.sharding import PartitionSpec as P

STEPS = 2
QS = 32
LANES = 128
GROUP = 6
VMEM_LIMIT = 60 * 1024 * 1024
LATTICE = [(q // 9 - 1, q // 3 % 3 - 1, q % 3 - 1) for q in range(27)]


def split(value):
    high = value.astype(jnp.bfloat16)
    low = (value - high.astype(jnp.float32)).astype(jnp.bfloat16)
    return high, low


def dot(a, b):
    return jnp.dot(a, b, preferred_element_type=jnp.float32)


def lane_iota(rows):
    return lax.broadcasted_iota(jnp.int32, (rows, LANES), 1)


def make_weights(w_in, w_mid, w_out, one, two, three):
    hidden = w_mid.shape[0]
    high, low = split(jnp.concatenate([w_in[...], jnp.zeros((hidden, QS - 27), jnp.float32)], axis=1))
    one[...] = jnp.concatenate([high, high, low], axis=1)
    high, low = split(w_mid[...])
    two[...] = jnp.concatenate(
        [jnp.concatenate([high, high], axis=1), jnp.concatenate([low, jnp.zeros_like(low)], axis=1)], axis=0
    )
    high, low = split(jnp.concatenate([w_out[...], jnp.zeros((QS - 27, hidden), jnp.float32)], axis=0))
    three[...] = jnp.concatenate(
        [jnp.concatenate([high, high], axis=1), jnp.concatenate([low, jnp.zeros_like(low)], axis=1)], axis=0
    )


def primal_stream(post_ref, x_rows, y_sides, write, z_depth):
    rows_x, rows_y = post_ref.shape[1], 8
    lane = lane_iota(rows_x)
    at_y = lane % rows_y
    last_z = (z_depth - 1) * rows_y
    for q, (ex, ey, ez) in enumerate(LATTICE):
        own = post_ref[q]
        if ex == 1:
            own = jnp.concatenate([x_rows[0, q - 18 : q - 17, :], own[: rows_x - 1]], axis=0)
        elif ex == -1:
            own = jnp.concatenate([own[1:], x_rows[1, q : q + 1, :]], axis=0)
        if ey != 0:
            j = (ex + 1) * 3 + ez + 1
            side = y_sides[0 if ey == 1 else 1, j, 1 - ex : 1 - ex + rows_x, :]
            if ey == 1:
                own = jnp.where(at_y == 0, pltpu.roll(side, LANES - rows_y + 1, 1), pltpu.roll(own, 1, 1))
            else:
                own = jnp.where(at_y == rows_y - 1, pltpu.roll(side, rows_y - 1, 1), pltpu.roll(own, LANES - 1, 1))
        if ez == 1:
            own = jnp.where(lane < rows_y, post_ref[26 - q], pltpu.roll(own, rows_y, 1))
        elif ez == -1:
            own = jnp.where(lane >= last_z, post_ref[26 - q], pltpu.roll(own, LANES - rows_y, 1))
        write(q, own)


def stream_rows(before, x_rows, sides, write):
    rows_x, pairs = before.shape[0], before.shape[1]
    rows_y = 8
    lane = lane_iota(rows_y)
    left = lane < LANES // 2
    at_y = lax.broadcasted_iota(jnp.int32, (rows_y, LANES), 0)
    def one_row(x, edge):
        for q, (ex, ey, ez) in enumerate(LATTICE):
            parts = []
            for pair in range(pairs):
                if edge == -1 and ex == 1:
                    value = x_rows[0, q - 18, pair]
                elif edge == 1 and ex == -1:
                    value = x_rows[1, q, pair]
                else:
                    value = before[x - ex, pair, q * rows_y : (q + 1) * rows_y, :]
                if ey != 0:
                    j = (ex + 1) * 3 + ez + 1
                    side = sides[0 if ey == 1 else 1, j, pair, pl.ds(x - ex + 1, 1), :]
                    if ey == 1:
                        value = jnp.where(at_y == 0, side, pltpu.roll(value, 1, 0))
                    else:
                        value = jnp.where(at_y == rows_y - 1, side, pltpu.roll(value, rows_y - 1, 0))
                parts.append(value)
            if ez != 0:
                turned = [pltpu.roll(part, LANES // 2, 1) for part in parts]
                mirror = 26 - q
                if ez == 1:
                    wall = before[x, 0, mirror * rows_y : (mirror + 1) * rows_y, :]
                    parts = [jnp.where(left, turned[p - 1] if p else wall, turned[p]) for p in range(pairs)]
                else:
                    wall = before[x, pairs - 1, mirror * rows_y : (mirror + 1) * rows_y, :]
                    parts = [jnp.where(left, turned[p], turned[p + 1] if p + 1 < pairs else wall) for p in range(pairs)]
            write(x, q, parts)

    one_row(0, -1)

    def inner(x, carry):
        one_row(x, 0)
        return carry

    lax.fori_loop(1, rows_x - 1, inner, 0)
    one_row(rows_x - 1, 1)


def primal_collide(state_ref, biases, post_ref, slope_one_ref, slope_two_ref, one, two, three):
    bias_in, bias_mid, bias_out = biases
    rows_x = post_ref.shape[1]
    hidden = two.shape[0] // 2

    def row(x, carry):
        cell = state_ref[pl.ds(x, QS, stride=rows_x), :]
        high, low = split(cell)
        act_one = jnp.tanh(dot(one[...], jnp.concatenate([high, low, high], axis=0)) + bias_in)
        high, low = split(act_one)
        second = dot(two[...], jnp.concatenate([high, low], axis=0))
        act_two = jnp.tanh(second[:hidden] + second[hidden:] + bias_mid)
        high, low = split(act_two)
        moved = dot(three[...], jnp.concatenate([high, low], axis=0))
        slope_one_ref[x] = 1.0 - act_one * act_one
        slope_two_ref[x] = 1.0 - act_two * act_two
        state_ref[pl.ds(x, QS, stride=rows_x), :] = cell + moved[:QS] + moved[QS:] + bias_out
        return carry

    lax.fori_loop(0, rows_x, row, 0, unroll=4)
    for q in range(27):
        post_ref[q] = state_ref[q * rows_x : (q + 1) * rows_x, :]


def collide_columns(x, columns, state, post, slope_one, slope_two, one, two, three):
    rows_y = 8
    hidden = two.shape[0] // 2
    half = lane_iota(hidden) < LANES // 2
    s_one, s_two = slope_one[x], slope_two[x]

    def scale(slopes, y, pair):
        left = slopes[:, 2 * pair * rows_y + y : 2 * pair * rows_y + y + 1]
        right = slopes[:, (2 * pair + 1) * rows_y + y : (2 * pair + 1) * rows_y + y + 1]
        return jnp.where(half, left, right)

    for start in range(0, len(columns), GROUP):
        here = columns[start : start + GROUP]
        cell = jnp.concatenate([state[x, pair, pl.ds(y, QS, stride=rows_y), :] for y, pair in here], axis=1)
        high, low = split(cell)
        lifted = dot(one[...], jnp.concatenate([high, low, high], axis=0))
        high, low = split(lifted * jnp.concatenate([scale(s_one, y, pair) for y, pair in here], axis=1))
        mixed = dot(two[...], jnp.concatenate([high, low], axis=0))
        mixed = mixed[:hidden] + mixed[hidden:]
        high, low = split(mixed * jnp.concatenate([scale(s_two, y, pair) for y, pair in here], axis=1))
        moved = dot(three[...], jnp.concatenate([high, low], axis=0))
        result = cell + moved[:QS] + moved[QS:]
        for i, (y, pair) in enumerate(here):
            post[x, pair, pl.ds(y, QS, stride=rows_y), :] = result[:, i * LANES : (i + 1) * LANES]


def exchange_and_collide(cell_state, state, weights, inflow, outs, scratch):
    w_in, b_in, w_mid, b_mid, w_out, b_out = weights
    cell_inflow, sens_inflow = inflow
    cell_post, cell_rows, cell_sides, post, x_rows, sides = outs
    (slope_one, slope_two, one, two, three, cell_edge, cell_face, edge, face,
     cell_edge_in, cell_face_in, cell_corner_in, edge_in, face_in, corner_in, send_sem, recv_sem) = scratch
    rows_x, pairs, rows_y = state.shape[0], state.shape[1], 8
    column, columns_x = lax.axis_index("gx"), lax.axis_size("gx")
    line, lines = lax.axis_index("gy"), lax.axis_size("gy")

    def at(dx, dy):
        return (lax.rem(column + dx + columns_x, columns_x), lax.rem(line + dy + lines, lines))

    barrier = pltpu.get_barrier_semaphore()
    for dx in (-1, 0, 1):
        for dy in (-1, 0, 1):
            if dx or dy:
                pl.semaphore_signal(barrier, inc=1, device_id=at(dx, dy), device_id_type=pl.DeviceIdType.MESH)

    copies = []

    def send(source, target, dx, dy):
        i = len(copies)
        copy = pltpu.make_async_remote_copy(
            src_ref=source, dst_ref=target, send_sem=send_sem.at[i], recv_sem=recv_sem.at[i],
            device_id=at(dx, dy), device_id_type=pl.DeviceIdType.MESH,
        )
        copy.start()
        copies.append(copy)

    make_weights(w_in, w_mid, w_out, one, two, three)
    def upright(bias):
        return jnp.transpose(jnp.broadcast_to(bias, (LANES, LANES)))

    out_bias = jnp.concatenate([b_out[...], jnp.zeros((1, LANES - 27), jnp.float32)], axis=1)
    biases = (upright(b_in[...]), upright(b_mid[...]), upright(out_bias)[:QS])
    primal_collide(cell_state, biases, cell_post, slope_one, slope_two, one, two, three)
    cell_edge[0] = cell_state[pl.ds(0, 16, stride=rows_x), :]
    cell_edge[1, :9] = cell_state[pl.ds(18 * rows_x + rows_x - 1, 9, stride=rows_x), :]
    cell_edge[1, 9:] = jnp.zeros((7, LANES), jnp.float32)
    for ex in range(3):
        for ez in range(3):
            cell_face[1, ex * 3 + ez] = cell_post[ex * 9 + 6 + ez]
            cell_face[0, ex * 3 + ez] = cell_post[ex * 9 + ez]

    inner = [(y, pair) for y in range(1, rows_y - 1) for pair in range(pairs)]
    outer = [(y, pair) for y in (0, rows_y - 1) for pair in range(pairs)]

    def outer_row(x, carry):
        collide_columns(x, outer, state, post, slope_one, slope_two, one, two, three)
        return carry

    def inner_row(x, carry):
        collide_columns(x, inner, state, post, slope_one, slope_two, one, two, three)
        return carry

    def end_row(i, carry):
        return inner_row(i * (rows_x - 1), carry)

    lax.fori_loop(0, rows_x, outer_row, 0, unroll=4)
    lax.fori_loop(0, 2, end_row, 0)
    stride = pairs * QS * rows_y
    flat = post.reshape(rows_x * stride, LANES)
    for pair in range(pairs):
        for ex in range(3):
            for ez in range(3):
                q = ex * 9 + 6 + ez
                face[1, ex * 3 + ez, pair] = flat[pl.ds((pair * QS + q + 1) * rows_y - 1, rows_x, stride=stride), :]
                q = ex * 9 + ez
                face[0, ex * 3 + ez, pair] = flat[pl.ds((pair * QS + q) * rows_y, rows_x, stride=stride), :]
        for j in range(9):
            edge[0, j, pair] = post[0, pair, j * rows_y : (j + 1) * rows_y, :]
            edge[1, j, pair] = post[rows_x - 1, pair, (18 + j) * rows_y : (19 + j) * rows_y, :]

    pl.semaphore_wait(barrier, 8)
    send(face.at[1], face_in.at[0], 0, 1)
    send(face.at[0], face_in.at[1], 0, -1)
    send(edge.at[1], edge_in.at[0], 1, 0)
    send(edge.at[0], edge_in.at[1], -1, 0)
    send(edge.at[1, 6:9], corner_in.at[0], 1, 1)
    send(edge.at[0, 6:9], corner_in.at[1], -1, 1)
    send(edge.at[1, 0:3], corner_in.at[2], 1, -1)
    send(edge.at[0, 0:3], corner_in.at[3], -1, -1)
    send(cell_face.at[1], cell_face_in.at[0], 0, 1)
    send(cell_face.at[0], cell_face_in.at[1], 0, -1)
    send(cell_edge.at[1], cell_edge_in.at[0], 1, 0)
    send(cell_edge.at[0], cell_edge_in.at[1], -1, 0)
    send(cell_edge.at[1], cell_corner_in.at[0], 1, 1)
    send(cell_edge.at[0], cell_corner_in.at[1], -1, 1)
    send(cell_edge.at[1], cell_corner_in.at[2], 1, -1)
    send(cell_edge.at[0], cell_corner_in.at[3], -1, -1)

    lax.fori_loop(1, rows_x - 1, inner_row, 0)
    for copy in copies:
        copy.wait()

    first, last = column == 0, column == columns_x - 1
    end = rows_x + 1
    cell_rows[0] = jnp.where(first, cell_inflow[1], cell_edge_in[0])
    cell_rows[1] = jnp.where(last, cell_state[pl.ds(rows_x - 1, 16, stride=rows_x), :], cell_edge_in[1])
    for j in range(9):
        for way in range(2):
            cell_sides[way, j, 1:end] = cell_face_in[way, j]
        for pair in range(pairs):
            own = post[rows_x - 1, pair, j * rows_y : (j + 1) * rows_y, :]
            x_rows[0, j, pair] = jnp.where(first, sens_inflow[1, j, pair], edge_in[0, j, pair])
            x_rows[1, j, pair] = jnp.where(last, own, edge_in[1, j, pair])
            for way in range(2):
                sides[way, j, pair, 1:end] = face_in[way, j, pair]
    for way, take in ((0, 6), (1, 0)):
        y = rows_y - 1 if way == 0 else 0
        for i in range(3):
            k = take + i
            cell_sides[way, 6 + i, 0:1] = jnp.where(
                first, cell_inflow[2 * way, k : k + 1, :], cell_corner_in[2 * way, k : k + 1, :])
            cell_sides[way, i, end : end + 1] = jnp.where(
                last, cell_face_in[way, i, rows_x - 1 :, :], cell_corner_in[2 * way + 1, k : k + 1, :])
            for pair in range(pairs):
                sides[way, 6 + i, pair, 0:1] = jnp.where(
                    first, sens_inflow[2 * way, k, pair, y : y + 1, :], corner_in[2 * way, i, pair, y : y + 1, :])
                sides[way, i, pair, end : end + 1] = jnp.where(
                    last, face_in[way, i, pair, rows_x - 1 :, :], corner_in[2 * way + 1, i, pair, y : y + 1, :])


def first_step(cells, tangent, cell_inflow, sens_inflow, w_in, b_in, w_mid, b_mid, w_out, b_out, *rest):
    outs, (cell_state, state), scratch = rest[:6], rest[6:8], rest[8:]
    rows_x, pairs = state.shape[0], state.shape[1]
    cell_state[27 * rows_x :, :] = jnp.zeros((5 * rows_x, LANES), jnp.float32)
    for q in range(27):
        cell_state[q * rows_x : (q + 1) * rows_x, :] = cells[q]

    def load(x, carry):
        for pair in range(pairs):
            for q in range(27):
                state[x, pair, q * 8 : (q + 1) * 8, :] = tangent[q, x, :, pair * LANES : (pair + 1) * LANES]
            state[x, pair, 27 * 8 :, :] = jnp.zeros((5 * 8, LANES), jnp.float32)
        return carry

    lax.fori_loop(0, rows_x, load, 0)
    weights = (w_in, b_in, w_mid, b_mid, w_out, b_out)
    exchange_and_collide(cell_state, state, weights, (cell_inflow, sens_inflow), outs, scratch)


def next_step(z_depth, cells, cell_rows, cell_sides, before, x_rows, sides, cell_inflow, sens_inflow,
              w_in, b_in, w_mid, b_mid, w_out, b_out, *rest):
    outs, (cell_state, state), scratch = rest[:6], rest[6:8], rest[8:]
    rows_x, pairs = state.shape[0], state.shape[1]
    cell_state[27 * rows_x :, :] = jnp.zeros((5 * rows_x, LANES), jnp.float32)

    def keep(q, value):
        cell_state[q * rows_x : (q + 1) * rows_x, :] = value

    primal_stream(cells, cell_rows, cell_sides, keep, z_depth)

    def write(x, q, parts):
        for pair in range(pairs):
            state[x, pair, q * 8 : (q + 1) * 8, :] = parts[pair]
            if q == 0:
                state[x, pair, 27 * 8 :, :] = jnp.zeros((5 * 8, LANES), jnp.float32)

    stream_rows(before, x_rows, sides, write)
    weights = (w_in, b_in, w_mid, b_mid, w_out, b_out)
    exchange_and_collide(cell_state, state, weights, (cell_inflow, sens_inflow), outs, scratch)


def last_step(z_depth, probe_cells, probe_counts, cells, cell_rows, cell_sides, before, x_rows, sides, primal_out, out, rows_out, observed):
    pairs = before.shape[1]
    rows_y = 8
    sums = {}

    def write(x, q, parts):
        vector = LATTICE[q]
        for pair in range(pairs):
            out[q, x, :, pair * LANES : (pair + 1) * LANES] = parts[pair]
            held = sums.setdefault((pair,), [None] * 4) if q else sums.__setitem__((pair,), [None] * 4) or sums[(pair,)]
            for m, factor in enumerate((1,) + vector):
                if factor == 0:
                    continue
                if held[m] is None:
                    held[m] = parts[pair] if factor == 1 else -parts[pair]
                else:
                    held[m] = held[m] + parts[pair] if factor == 1 else held[m] - parts[pair]
            if q == 26:
                for m in range(4):
                    observed[m, pair, pl.ds(pl.multiple_of(x * rows_y, rows_y), rows_y), :] = held[m]

    def keep(q, value):
        primal_out[q] = value

    primal_stream(cells, cell_rows, cell_sides, keep, z_depth)
    stream_rows(before, x_rows, sides, write)
    peers, slots = probe_cells.shape
    left = lane_iota(1) < LANES // 2

    def probe(peer, carry):
        for slot in range(slots):
            cell = jnp.clip(probe_cells[peer, slot], 0, observed.shape[2] * z_depth - 1)
            place, z = cell // z_depth, cell % z_depth
            pair, odd = z // 2, z % 2
            live = slot < probe_counts[0, peer]
            rows = [observed[m, pair, pl.ds(place, 1), :] for m in range(4)]
            turned = [pltpu.roll(r, LANES // 2, 1) for r in rows]
            for m in (0, 2):
                low = jnp.where(odd == 1, turned[m], rows[m])
                high = jnp.where(odd == 1, rows[m + 1], turned[m + 1])
                value = jnp.where(left, low, high)
                rows_out[peer, slot : slot + 1, m * 64 : m * 64 + LANES] = jnp.where(live, value, 0.0)
        return carry

    lax.fori_loop(0, peers, probe, 0, unroll=2)


def shape(*dims):
    return jax.ShapeDtypeStruct(dims, jnp.float32)


def call(body, outs, scratch=(), collective=None, **more):
    params = {} if collective is None else {"collective_id": collective, "has_side_effects": True}
    return pl.pallas_call(
        body,
        out_shape=outs,
        scratch_shapes=list(scratch),
        compiler_params=pltpu.CompilerParams(vmem_limit_bytes=VMEM_LIMIT, **params),
        **more,
    )


def near_inflow(values, row_at, rows_y):
    around = jnp.concatenate([values[:, -rows_y:], values, values[:, :rows_y]], axis=1)
    return lax.dynamic_slice_in_dim(around, row_at, 3 * rows_y, 1).reshape(9, 3, rows_y, -1)


def on_device(primal_pops, tangent_pops, inflow_pops, inflow_sens, w_in, b_in, w_mid, b_mid, w_out, b_out,
              probe_cells, probe_counts):
    rows_x, rows_y, z_depth = primal_pops.shape[1:]
    width = tangent_pops.shape[3]
    pairs = width // LANES
    hidden = w_in.shape[0]
    row_at = lax.axis_index("gy") * rows_y

    weights = (w_in, b_in[None], w_mid, b_mid[None], w_out, b_out[None])
    tall = ((0, 0), (0, 0), (0, LANES - z_depth * rows_y))
    cells = jnp.pad(jnp.swapaxes(primal_pops, 2, 3).reshape(27, rows_x, z_depth * rows_y), tall)
    inflow = jnp.transpose(near_inflow(inflow_pops, row_at, rows_y), (1, 0, 3, 2)).reshape(3, 9, z_depth * rows_y)
    inflow = jnp.pad(inflow, ((0, 0), (0, 7), (0, LANES - z_depth * rows_y)))
    sens = near_inflow(inflow_sens, row_at, rows_y).reshape(9, 3, rows_y, pairs, LANES)
    sens = jnp.transpose(sens, (1, 0, 3, 2, 4))

    tall_x = rows_x + 8
    outs = (
        shape(27, rows_x, LANES),
        shape(2, 16, LANES),
        shape(2, 9, tall_x, LANES),
        shape(rows_x, pairs, QS * rows_y, LANES),
        shape(2, 9, pairs, rows_y, LANES),
        shape(2, 9, pairs, tall_x, LANES),
    )

    def room(*dims, kind=jnp.float32):
        return pltpu.VMEM(dims, kind)

    scratch = [
        room(QS * rows_x, LANES),
        room(rows_x, pairs, QS * rows_y, LANES),
        room(rows_x, hidden, LANES),
        room(rows_x, hidden, LANES),
        room(hidden, 3 * QS, kind=jnp.bfloat16),
        room(2 * hidden, 2 * hidden, kind=jnp.bfloat16),
        room(2 * QS, 2 * hidden, kind=jnp.bfloat16),
        room(2, 16, LANES),
        room(2, 9, rows_x, LANES),
        room(2, 9, pairs, rows_y, LANES),
        room(2, 9, pairs, rows_x, LANES),
        room(2, 16, LANES),
        room(2, 9, rows_x, LANES),
        room(4, 16, LANES),
        room(2, 9, pairs, rows_y, LANES),
        room(2, 9, pairs, rows_x, LANES),
        room(4, 3, pairs, rows_y, LANES),
        pltpu.SemaphoreType.DMA((16,)),
        pltpu.SemaphoreType.DMA((16,)),
    ]
    held = call(first_step, outs, scratch, 1)(cells, tangent_pops, inflow, sens, *weights)
    for step in range(1, STEPS):
        held = call(functools.partial(next_step, z_depth), outs, scratch, 1 + step)(*held, inflow, sens, *weights)
    peers, slots = probe_cells.shape[1:]
    smem = pl.BlockSpec(memory_space=pltpu.SMEM)
    vmem = pl.BlockSpec(memory_space=pltpu.VMEM)
    primal, tangent, jac = call(
        functools.partial(last_step, z_depth),
        (
            shape(27, rows_x, LANES),
            shape(27, rows_x, rows_y, width),
            shape(peers, slots, 4 * width // z_depth),
        ),
        [room(4, pairs, rows_x * rows_y, LANES)],
        in_specs=[smem, smem] + [vmem] * 6,
    )(probe_cells[0], probe_counts, *held)
    primal = jnp.swapaxes(primal[:, :, : z_depth * rows_y].reshape(27, rows_x, z_depth, rows_y), 2, 3)
    jac = lax.all_to_all(jac[None], ("gx", "gy"), split_axis=1, concat_axis=1, tiled=True)
    return primal, tangent, jac


def solution(mesh):
    both = P(("gx", "gy"))
    split_xy = P(None, "gx", "gy", None)
    return jax.shard_map(
        on_device,
        mesh=mesh,
        in_specs=(split_xy, split_xy) + (P(),) * 8 + (both, both),
        out_specs=(split_xy, split_xy, both),
        check_vma=False,
    )
```
